32 devices in a mesh: lat: 4 (over x, core), lon: 8 (over z, y).
Axes of the slice: x: 2, y: 2, z: 4, core: 2. Of those that a mesh axis runs over, the one named last changes fastest.
Arguments:
- field: bfloat16 [64, 256, 1024], P('lat', 'lon'), may hold values from -600 to 600
- norm_gain: float32 [1024], replicated, may hold values from 0.1 to 1.9
- w_qkv: bfloat16 [1024, 3072], replicated, may hold values from -2 to 2
- w_out: bfloat16 [1024, 1024], replicated, may hold values from -0.1875 to 0.1875
- block_cols: int32 [4, 4], replicated, may hold values from 1 to 7, as said below
- antipode: int32 [256], P('lon'), may hold values from 0 to 255, as said below
Outputs:
- update: bfloat16 [64, 256, 1024], P('lat', 'lon')
The draws below stay inside these ranges and needn't reach their ends.
Inputs may be any that keep to these rules, and one draw needn't show every extreme that they name: `block_cols`: each row lists 4 different blocks b with |b - 4 - row| <= 3. A permutation of the longitudes; antipode[l] // 32 equals (l // 32 + 256 // 64) modulo 256 // 32.
All inputs are finite; a program needn't handle non-finite values.
Results may differ from the reference program's by a relative error of at most 0.005.
The reference program's roundings to bfloat16 on the way count: a program that leaves them out, or rounds other values in their place, can miss the bound.
Values may be sent and summed in bfloat16 or wider, within the bound.
A program may use at most 128 MiB of HBM per device.

```python
import jax
import jax.numpy as jnp
from jax import lax

D = 1024
HEADS = 16
HD = 64
HZ = 8
CAP = 32
BM = 8
KSEL = 4
BANDB = 3
L_DEV = 32
CYCLES = 64
LON = 256
NB = 8
QB = 4


def draw_field(key, part):
    key_base, key_rows, key_cols = jax.random.split(key, 3)
    row_scale = jnp.exp(jax.random.uniform(key_rows, (CYCLES, LON, 1), jnp.float32) * jnp.log(10.0))
    col_scale = jnp.exp(jax.random.uniform(key_cols, (D,), jnp.float32) * jnp.log(10.0))
    sample = jax.random.normal(key_base, (CYCLES, LON, D), jnp.float32)
    return jnp.clip(sample * row_scale * col_scale, -600.0, 600.0).astype(jnp.bfloat16)


def draw_w_qkv(key, part):
    key_base = jax.random.fold_in(key, 0)
    sample = jnp.clip(jax.random.normal(key_base, (D, 3 * D), jnp.float32), -6.0, 6.0) * D ** (-0.5)
    return jnp.clip(sample, -2.0, 2.0).astype(jnp.bfloat16)


def draw_block_cols(key, part):
    band_span = 2 * BANDB + 1
    offsets = jnp.arange(band_span, dtype=jnp.int32) - BANDB
    row_ids = jnp.arange(QB, dtype=jnp.int32)
    blocks = QB + row_ids[:, None] + offsets[None, :]
    in_range = (blocks >= 0) & (blocks < NB)
    scores = jax.random.randint(key, (QB, band_span), 0, 1000, dtype=jnp.int32) * band_span + offsets[None, :] + BANDB
    scores = jnp.where(in_range, scores, -1)
    chosen = lax.top_k(scores, KSEL)[1]
    return jnp.take_along_axis(blocks, chosen, axis=1).astype(jnp.int32)


def draw_antipode(key, part):
    block_count = LON // L_DEV

    def one_block(block_index):
        shuffled = jax.random.permutation(jax.random.fold_in(key, block_index), L_DEV)
        target = (block_index + block_count // 2) % block_count
        return target * L_DEV + shuffled
    return jax.vmap(one_block)(jnp.arange(block_count, dtype=jnp.int32)).reshape(LON).astype(jnp.int32)


def centred(stream_key, shape, width, reach, kind=jnp.bfloat16):
    result = jax.random.normal(stream_key, shape, jnp.float32) * width
    return jnp.minimum(jnp.maximum(result, -reach), reach).astype(kind)


def setup_inputs(seed: int = 0) -> dict:
    key_of = jax.random.split(jax.random.key(seed), 7)
    return {
        "field": draw_field(jax.random.fold_in(key_of[6], 71), 0),
        "norm_gain": jnp.clip(1.0 + 0.18 * jax.random.normal(key_of[1], (D,), jnp.float32), 0.1, 1.9),
        "w_qkv": draw_w_qkv(jax.random.fold_in(key_of[6], 71), 0),
        "w_out": centred(key_of[3], (D, D), D ** -0.5, 0.1875),
        "block_cols": draw_block_cols(jax.random.fold_in(key_of[6], 71), 0),
        "antipode": draw_antipode(jax.random.fold_in(key_of[6], 71), 0),
    }


epsilon = 1e-06

def softmax_rows(scores):
    row_max = lax.optimization_barrier(jnp.max(scores, axis=-1, keepdims=True))
    exponent = jnp.exp(scores - row_max)
    return (exponent / lax.optimization_barrier(jnp.sum(exponent, axis=-1, keepdims=True))).astype(jnp.bfloat16)

def rms_normed(field, norm_gain):
    values = field.astype(jnp.float32)
    scaled = values * lax.rsqrt(lax.optimization_barrier(jnp.mean(values * values, axis=-1, keepdims=True)) + epsilon)
    return (scaled * norm_gain).astype(jnp.bfloat16)

def reference(field, norm_gain, w_qkv, w_out, block_cols, antipode):
    cycle_count, lon_count, channels = field.shape
    normed = rms_normed(field, norm_gain)
    projected = jnp.dot(normed.reshape(cycle_count * lon_count, channels), w_qkv, preferred_element_type=jnp.float32)
    projected = projected.astype(jnp.bfloat16).reshape(cycle_count, lon_count, 3, HEADS, HD)
    score_scale = HD ** (-0.5)

    def cycle_attend(triple):
        query_rows, key_rows, value_rows = triple
        scores = jnp.einsum('qhd,khd->hqk', query_rows.astype(jnp.float32), key_rows.astype(jnp.float32)) * score_scale
        soft_weights = softmax_rows(scores)
        return jnp.einsum('hqk,khd->qhd', soft_weights.astype(jnp.float32), value_rows.astype(jnp.float32)).astype(jnp.bfloat16)
    zonal_out = lax.map(cycle_attend, (projected[:, :, 0, :HZ], projected[:, :, 1, :HZ], projected[:, :, 2, :HZ]))
    pieces = []
    for polar_cap in range(2):
        cap_block = projected[polar_cap * CAP:(polar_cap + 1) * CAP, :, :, HZ:]
        across = jnp.take(cap_block, antipode, axis=1)[::-1]
        column = jnp.concatenate([across, cap_block], axis=0)
        for block_row in range(QB):
            query_rows = cap_block[block_row * BM:(block_row + 1) * BM, :, 0]
            picked_rows = (block_cols[block_row][:, None] * BM + jnp.arange(BM, dtype=jnp.int32)[None, :]).reshape(-1)
            chosen = jnp.take(column, picked_rows.astype(jnp.int32), axis=0)
            scores = jnp.einsum('qlhd,klhd->lhqk', query_rows.astype(jnp.float32), chosen[:, :, 1].astype(jnp.float32)) * score_scale
            soft_weights = softmax_rows(scores)
            pieces.append(jnp.einsum('lhqk,klhd->qlhd', soft_weights.astype(jnp.float32), chosen[:, :, 2].astype(jnp.float32)).astype(jnp.bfloat16))
    meridional = jnp.concatenate(pieces, axis=0)
    attended = jnp.concatenate([zonal_out, meridional], axis=2).reshape(cycle_count * lon_count, channels)
    update = jnp.dot(attended, w_out, preferred_element_type=jnp.float32).astype(jnp.bfloat16)
    return update.reshape(cycle_count, lon_count, channels)
```

```python
import functools

import jax
import jax.numpy as jnp
from jax import lax
from jax.experimental import pallas as pl
from jax.experimental.pallas import tpu as pltpu
from jax.sharding import PartitionSpec as P

HEADS = 16
HD = 64
HZ = 8
BM = 8


epsilon = 1e-06


def shifted(shard, axis, by):
    devices = lax.axis_size(axis)
    return lax.ppermute(shard, axis, [(i, (i + by) % devices) for i in range(devices)])


def from_partner(value, axis, distance):
    mask = 2**distance
    pairs = [(source, source ^ mask) for source in range(lax.axis_size(axis))]
    return lax.ppermute(value, axis, pairs)


def softmax_rows(scores):
    row_max = jnp.max(scores, axis=-1, keepdims=True)
    exponent = jnp.exp(scores - row_max)
    return (exponent / jnp.sum(exponent, axis=-1, keepdims=True)).astype(jnp.bfloat16)


def zonal_attend(query_rows, key_rows, value_rows):
    item_count, length, pair_width = query_rows.shape
    score_scale = HD ** (-0.5)
    query_heads = query_rows.reshape(item_count, length, 2, HD)
    key_heads = key_rows.reshape(item_count, length, 2, HD)
    value_heads = value_rows.reshape(item_count, length, 2, HD)
    block_rows = min(512, length)
    pieces = []
    for first_row in range(0, length, block_rows):
        query_block = query_heads[:, first_row : first_row + block_rows]
        scores = (
            jnp.einsum(
                "iqhd,ikhd->ihqk", query_block, key_heads, preferred_element_type=jnp.float32
            )
            * score_scale
        )
        soft_weights = softmax_rows(scores)
        result = jnp.einsum(
            "ihqk,ikhd->iqhd", soft_weights, value_heads, preferred_element_type=jnp.float32
        )
        pieces.append(result.astype(jnp.bfloat16))
    return jnp.concatenate(pieces, axis=1).reshape(item_count, length, pair_width)


def on_device(field, norm_gain, w_qkv, w_out, block_cols, antipode):
    cycle_count, lon_count, channels = field.shape
    column_heads = HEADS - HZ
    pair_count = HZ // 2
    zonal_width = HZ * HD
    score_scale = HD ** (-0.5)
    values = field.astype(jnp.float32)
    scaled = values * lax.rsqrt(jnp.mean(values * values, axis=-1, keepdims=True) + epsilon)
    normed = (scaled * norm_gain).astype(jnp.bfloat16)
    weight_split = w_qkv.reshape(channels, 3, channels)
    zonal_weight = weight_split[:, :, :zonal_width].reshape(channels, 3, pair_count, 2 * HD)
    column_weight = weight_split[:, :, zonal_width:]
    zonal_part = jnp.einsum(
        "rld,dtpc->trplc", normed, zonal_weight, preferred_element_type=jnp.float32
    )
    zonal_part = zonal_part.astype(jnp.bfloat16).reshape(
        3, cycle_count * pair_count, lon_count, 2 * HD
    )
    column_proj = jnp.einsum(
        "rld,dtc->rltc", normed, column_weight, preferred_element_type=jnp.float32
    ).astype(jnp.bfloat16)
    query_all, key_all, value_all = (
        lax.all_to_all(zonal_part[0], "lon", split_axis=0, concat_axis=1, tiled=True),
        lax.all_to_all(zonal_part[1], "lon", split_axis=0, concat_axis=1, tiled=True),
        lax.all_to_all(zonal_part[2], "lon", split_axis=0, concat_axis=1, tiled=True),
    )
    zonal_items = zonal_attend(query_all, key_all, value_all)
    returned = lax.all_to_all(zonal_items, "lon", split_axis=1, concat_axis=0, tiled=True)
    zonal_out = returned.reshape(cycle_count, pair_count, lon_count, 2 * HD)
    cap_half = lax.axis_index("lat") % 2
    lon_devices = lax.axis_size("lon")
    merged = column_proj[:, :, 1:]

    def cap_order(own_rows, other_rows):
        return jnp.where(
            cap_half == 0,
            jnp.concatenate([own_rows, other_rows], axis=0),
            jnp.concatenate([other_rows, own_rows], axis=0),
        )

    far_own = shifted(merged, "lon", lon_devices // 2)
    partner, far_partner = from_partner((merged, far_own), "lat", 0)
    cap_rows = cap_order(merged, partner)
    far_side = cap_order(far_own, far_partner)
    across = jnp.take(far_side, antipode % lon_count, axis=1)[::-1]
    column = jnp.concatenate([across, cap_rows], axis=0)
    block_total = column.shape[0] // BM
    column = column.reshape(block_total, BM, lon_count, 2, column_heads, HD)
    picks_per_row = block_cols.shape[1]
    local_blocks = cycle_count // BM
    pieces = []
    for local_block in range(local_blocks):
        block_row = cap_half * local_blocks + local_block
        picked = lax.dynamic_index_in_dim(block_cols, block_row, 0, keepdims=False)
        chosen = jnp.take(column, picked, axis=0).reshape(
            picks_per_row * BM, lon_count, 2, column_heads, HD
        )
        query_block = column_proj[local_block * BM : (local_block + 1) * BM, :, 0]
        query_block = query_block.reshape(BM, lon_count, column_heads, HD)
        scores = (
            jnp.einsum(
                "qlhd,klhd->lhqk", query_block, chosen[:, :, 0], preferred_element_type=jnp.float32
            )
            * score_scale
        )
        soft_weights = softmax_rows(scores)
        result = jnp.einsum(
            "lhqk,klhd->qlhd", soft_weights, chosen[:, :, 1], preferred_element_type=jnp.float32
        )
        pieces.append(result.astype(jnp.bfloat16).reshape(BM, lon_count, column_heads * HD))
    meridional = jnp.concatenate(pieces, axis=0)
    zonal_rows_out = w_out[:zonal_width].reshape(pair_count, 2 * HD, channels)
    total = jnp.einsum(
        "rplc,pce->rle", zonal_out, zonal_rows_out, preferred_element_type=jnp.float32
    )
    total = total + jnp.einsum(
        "rlc,ce->rle", meridional, w_out[zonal_width:], preferred_element_type=jnp.float32
    )
    return total.astype(jnp.bfloat16)


GROUP = 4
MESH = pl.DeviceIdType.MESH


def places():
    lat, lon = lax.axis_index("lat"), lax.axis_index("lon")
    half, q = lon // GROUP, lon % GROUP
    return lat, lon, half, q


def exchange_kernel(x_ref, xz_ref, part_ref, far_ref, farpart_ref, send, recv, local):
    lat, lon, half, q = places()
    anti = (1 - half) * GROUP + q
    mate = lat + 1 - 2 * (lat % 2)
    rows = x_ref.shape[0] // GROUP

    def peer(k):
        return (q + k) % GROUP

    def chunk(ref, p):
        return ref.at[pl.ds(p * rows, rows)]

    def remote(src, dst, n, lat_id, lon_id):
        return pltpu.make_async_remote_copy(
            src_ref=src,
            dst_ref=dst,
            send_sem=send.at[n],
            recv_sem=recv.at[n],
            device_id=(lat_id, lon_id),
            device_id_type=MESH,
        )

    barrier = pltpu.get_barrier_semaphore()
    partners = [(lat, anti), (mate, lon)] + [(lat, half * GROUP + peer(k)) for k in (1, 2, 3)]
    for a, b in partners:
        pl.semaphore_signal(barrier, inc=1, device_id=(a, b), device_id_type=MESH)
    pl.semaphore_wait(barrier, len(partners))

    order = (1, 2, 3, 0)
    far = [remote(chunk(x_ref, peer(k)), chunk(far_ref, peer(k)), n, lat, anti) for n, k in enumerate(order)]
    near = [
        remote(chunk(x_ref, peer(k)), xz_ref.at[0, q], 3 + k, lat, half * GROUP + peer(k))
        for k in (1, 2, 3)
    ]
    pair = remote(x_ref, part_ref, 7, mate, lon)
    for copy in far + near + [pair]:
        copy.start()
    own = pltpu.make_async_copy(chunk(x_ref, q), xz_ref.at[0, q], local.at[0])
    own.start()
    later = []
    for n, k in enumerate(order):
        far[n].wait_recv()
        got = chunk(far_ref, peer(k))
        if k:
            on = remote(got, xz_ref.at[1, q], 7 + k, lat, half * GROUP + peer(k))
        else:
            on = pltpu.make_async_copy(got, xz_ref.at[1, q], local.at[1])
        on.start()
        across = remote(got, chunk(farpart_ref, peer(k)), 11 + n, mate, lon)
        across.start()
        later += [on, across]
    for copy in far:
        copy.wait_send()
    for copy in near + [pair, own] + later:
        copy.wait()


def exchange(field):
    cycles, lons, width = field.shape
    like = jax.ShapeDtypeStruct(field.shape, field.dtype)
    return pl.pallas_call(
        exchange_kernel,
        name="exchange",
        out_shape=(
            jax.ShapeDtypeStruct((2, GROUP, cycles // GROUP, lons, width), field.dtype),
            like,
            like,
            like,
        ),
        in_specs=[pl.BlockSpec(memory_space=pl.ANY)],
        out_specs=[pl.BlockSpec(memory_space=pl.ANY)] * 4,
        scratch_shapes=[
            pltpu.SemaphoreType.DMA((15,)),
            pltpu.SemaphoreType.DMA((15,)),
            pltpu.SemaphoreType.DMA((2,)),
        ],
        compiler_params=pltpu.CompilerParams(collective_id=0, has_side_effects=True),
    )(field)


def giveback_kernel(z_ref, out_ref, send, recv, local):
    lat, lon, half, q = places()
    rows = out_ref.shape[0] // GROUP
    barrier = pltpu.get_barrier_semaphore()
    peers = [(q + k) % GROUP for k in (1, 2, 3)]
    for p in peers:
        pl.semaphore_signal(barrier, inc=1, device_id=(lat, half * GROUP + p), device_id_type=MESH)
    pl.semaphore_wait(barrier, 3)
    mine = out_ref.at[pl.ds(q * rows, rows)]
    copies = [
        pltpu.make_async_remote_copy(
            src_ref=z_ref.at[p],
            dst_ref=mine,
            send_sem=send.at[n],
            recv_sem=recv.at[n],
            device_id=(lat, half * GROUP + p),
            device_id_type=MESH,
        )
        for n, p in enumerate(peers)
    ]
    copies.append(pltpu.make_async_copy(z_ref.at[q], mine, local))
    for copy in copies:
        copy.start()
    for copy in copies:
        copy.wait()


def giveback(zonal):
    group, rows, lons, width = zonal.shape
    return pl.pallas_call(
        giveback_kernel,
        name="giveback",
        out_shape=jax.ShapeDtypeStruct((group * rows, lons, width), zonal.dtype),
        in_specs=[pl.BlockSpec(memory_space=pl.ANY)],
        out_specs=pl.BlockSpec(memory_space=pl.ANY),
        scratch_shapes=[
            pltpu.SemaphoreType.DMA((3,)),
            pltpu.SemaphoreType.DMA((3,)),
            pltpu.SemaphoreType.DMA,
        ],
        compiler_params=pltpu.CompilerParams(collective_id=1, has_side_effects=True),
    )(zonal)


def norm_rows(x, gain):
    values = x.astype(jnp.float32)
    mean = jnp.mean(values * values, axis=-1, keepdims=True)
    return (values * lax.rsqrt(mean + epsilon) * gain).astype(jnp.bfloat16)


def mm(a, b):
    return jnp.dot(a, b, preferred_element_type=jnp.float32).astype(jnp.bfloat16)


def pair_attend(q, k, v, mask):
    rows = q.shape[0]
    first = lax.broadcasted_iota(jnp.int32, q.shape, 1) < HD
    q = q * jnp.asarray(HD ** (-0.5), q.dtype)
    zero = jnp.zeros_like(q)
    stacked = jnp.concatenate([jnp.where(first, q, zero), jnp.where(first, zero, q)], axis=0)
    scores = lax.dot_general(stacked, k, (((1,), (1,)), ((), ())), preferred_element_type=jnp.float32)
    if mask is not None:
        scores = jnp.where(mask, scores, -jnp.inf)
    exponent = jnp.exp(scores - jnp.max(scores, axis=-1, keepdims=True))
    weights = (exponent * (1.0 / jnp.sum(exponent, axis=-1, keepdims=True))).astype(jnp.bfloat16)
    out = jnp.dot(weights, v, preferred_element_type=jnp.float32)
    return jnp.where(first, out[:rows], out[rows:]).astype(jnp.bfloat16)


STEP = 256


def attend_kernel(
    slots_ref, x_ref, part_ref, far_ref, farpart_ref, xz_ref, gain_ref, w_ref, own_ref, ant_ref,
    zo_ref, col_ref, xn, kc, vc, qc, kz, vz, qz, oc,
):
    gain = gain_ref[...]
    tokens = x_ref.shape[0]
    width = x_ref.shape[1]
    part = HZ * HD

    def weight(which, side):
        first = which * width + side * part
        return w_ref[:, first : first + part]

    for s, (ref, order) in enumerate(
        ((x_ref, own_ref), (part_ref, own_ref), (far_ref, ant_ref), (farpart_ref, ant_ref))
    ):
        @pl.loop(0, tokens // 64)
        def _(i):
            at = pl.ds(pl.multiple_of(i * 64, 64), 64)
            xn[at, :] = norm_rows(ref[at, :], gain)

        @pl.loop(0, tokens // STEP)
        def _(i):
            at = pl.ds(pl.multiple_of(i * STEP, STEP), STEP)
            hit = lax.broadcasted_iota(jnp.int32, (STEP, tokens), 1) == order[at, :]
            placed = mm(jnp.where(hit, 1.0, 0.0).astype(jnp.bfloat16), xn[...])
            to = pl.ds(pl.multiple_of(s * tokens + i * STEP, STEP), STEP)
            kc[to, :] = mm(placed, weight(1, 1))
            vc[to, :] = mm(placed, weight(2, 1))
            if s == 0:
                qc[at, :] = mm(placed, weight(0, 1))

    @pl.loop(0, xz_ref.shape[0] // STEP)
    def _(i):
        for j in range(STEP // 64):
            at = pl.ds(pl.multiple_of(i * STEP + j * 64, 64), 64)
            xn[j * 64 : (j + 1) * 64, :] = norm_rows(xz_ref[at, :], gain)
        at = pl.ds(pl.multiple_of(i * STEP, STEP), STEP)
        placed = xn[0:STEP, :]
        kz[at, :] = mm(placed, weight(1, 0))
        vz[at, :] = mm(placed, weight(2, 0))

        @pl.when(i * STEP < tokens)
        def _():
            qz[at, :] = mm(placed, weight(0, 0))

    rows = BM * 8
    groups = tokens // (2 * rows)
    mask = (
        lax.broadcasted_iota(jnp.int32, (2 * rows, 4 * rows), 0) % 8
        == lax.broadcasted_iota(jnp.int32, (2 * rows, 4 * rows), 1) % 8
    )

    @pl.loop(0, 2 * groups)
    def _(n):
        block, g = n // groups, n % groups
        at = pl.ds(pl.multiple_of(n * rows, rows), rows)
        picks = [
            pl.ds(pl.multiple_of((slots_ref[block, m] * groups + g) * rows, rows), rows) for m in range(4)
        ]
        for p in range(part // 128):
            cols = slice(p * 128, (p + 1) * 128)
            k = jnp.concatenate([kc[pick, cols] for pick in picks], axis=0)
            v = jnp.concatenate([vc[pick, cols] for pick in picks], axis=0)
            oc[at, cols] = pair_attend(qc[at, cols], k, v, mask)

    @pl.loop(0, tokens // STEP)
    def _(i):
        at = pl.ds(pl.multiple_of(i * STEP, STEP), STEP)
        token = lax.broadcasted_iota(jnp.int32, (STEP, tokens), 0) + i * STEP
        place = lax.broadcasted_iota(jnp.int32, (STEP, tokens), 1)
        lons = 8 * groups
        cycle, l = token // lons, token % lons
        want = (((cycle // BM) * groups + l // 8) * BM + cycle % BM) * 8 + l % 8
        col_ref[at, :] = mm(jnp.where(want == place, 1.0, 0.0).astype(jnp.bfloat16), oc[...])

    lons = 8 * groups
    per = xz_ref.shape[0] // (2 * GROUP * lons)

    @pl.loop(0, per)
    def _(c):
        def gather(ref, cols, many):
            return jnp.concatenate(
                [ref[pl.ds(pl.multiple_of((m * per + c) * lons, lons), lons), cols] for m in range(many)],
                axis=0,
            )

        for p in range(part // 128):
            cols = slice(p * 128, (p + 1) * 128)
            out = pair_attend(
                gather(qz, cols, GROUP), gather(kz, cols, 2 * GROUP), gather(vz, cols, 2 * GROUP), None
            )
            for m in range(GROUP):
                to = pl.ds(pl.multiple_of((m * per + c) * lons, lons), lons)
                zo_ref[to, cols] = out[m * lons : (m + 1) * lons]


def attend(slots, x, part, far, farpart, xz, gain, w_qkv, own, ant):
    tokens, width = x.shape
    side = HZ * HD
    bf = jnp.bfloat16
    vmem = pl.BlockSpec(memory_space=pltpu.VMEM)
    return pl.pallas_call(
        attend_kernel,
        name="attend",
        out_shape=(jax.ShapeDtypeStruct((tokens, side), bf), jax.ShapeDtypeStruct((tokens, side), bf)),
        in_specs=[pl.BlockSpec(memory_space=pltpu.SMEM)] + [vmem] * 9,
        out_specs=[vmem, vmem],
        scratch_shapes=[
            pltpu.VMEM((tokens, width), bf),
            pltpu.VMEM((4 * tokens, side), bf),
            pltpu.VMEM((4 * tokens, side), bf),
            pltpu.VMEM((tokens, side), bf),
            pltpu.VMEM((2 * tokens, side), bf),
            pltpu.VMEM((2 * tokens, side), bf),
            pltpu.VMEM((tokens, side), bf),
            pltpu.VMEM((tokens, side), bf),
        ],
        compiler_params=pltpu.CompilerParams(vmem_limit_bytes=56 * 1024 * 1024),
    )(slots, x, part, far, farpart, xz, gain, w_qkv, own, ant)


def placement(block_cols, antipode, cycles, lons):
    cap_half = lax.axis_index("lat") % 2
    blocks = cycles // BM
    picks = lax.dynamic_slice_in_dim(block_cols, cap_half * blocks, blocks, 0)
    cap_block = jnp.where(picks >= 2 * blocks, picks - 2 * blocks, 2 * blocks - 1 - picks)
    slots = (
        jnp.where(picks >= 2 * blocks, 0, 2 * blocks)
        + jnp.where(cap_block // blocks == cap_half, 0, blocks)
        + cap_block % blocks
    )
    shape = (blocks, lons // 8, BM, 8)
    axis = [lax.broadcasted_iota(jnp.int32, shape, n) for n in range(4)]
    cycle = axis[0] * BM + axis[2]
    own = cycle * lons + axis[1] * 8 + axis[3]
    far = cycle * lons + (antipode % lons).reshape(1, lons // 8, 1, 8)
    return slots.astype(jnp.int32), own.reshape(-1, 1), far.reshape(-1, 1)


def on_device_halves(field, norm_gain, w_qkv, w_out, block_cols, antipode):
    cycles, lons, width = field.shape
    tokens = cycles * lons
    slots, own, ant = placement(block_cols, antipode, cycles, lons)
    xz, part, far, farpart = exchange(field)
    flat = [a.reshape(-1, width) for a in (field, part, far, farpart, xz)]
    zonal, column = attend(slots, *flat, norm_gain.reshape(1, width), w_qkv, own, ant)
    back = giveback(zonal.reshape(GROUP, cycles // GROUP, lons, HZ * HD)).reshape(tokens, HZ * HD)
    total = jnp.dot(back, w_out[: HZ * HD], preferred_element_type=jnp.float32)
    total = total + jnp.dot(column, w_out[HZ * HD :], preferred_element_type=jnp.float32)
    return total.astype(jnp.bfloat16).reshape(cycles, lons, width)


def solution(mesh):
    in_specs = (P("lat", "lon", None), P(), P(), P(), P(), P("lon"))
    out_specs = P("lat", "lon", None)
    halves = mesh.shape["lat"] == 4 and mesh.shape["lon"] == 2 * GROUP
    return jax.shard_map(
        on_device_halves if halves else on_device,
        mesh=mesh,
        in_specs=in_specs,
        out_specs=out_specs,
        check_vma=False,
    )
```

```python
import functools

import jax
import jax.numpy as jnp
from jax import lax
from jax.experimental import pallas as pl
from jax.experimental.pallas import tpu as pltpu
from jax.sharding import PartitionSpec as P

HEADS = 16
HD = 64
HZ = 8
BM = 8


epsilon = 1e-06


def shifted(shard, axis, by):
    devices = lax.axis_size(axis)
    return lax.ppermute(shard, axis, [(i, (i + by) % devices) for i in range(devices)])


def from_partner(value, axis, distance):
    mask = 2**distance
    pairs = [(source, source ^ mask) for source in range(lax.axis_size(axis))]
    return lax.ppermute(value, axis, pairs)


def softmax_rows(scores):
    row_max = jnp.max(scores, axis=-1, keepdims=True)
    exponent = jnp.exp(scores - row_max)
    return (exponent / jnp.sum(exponent, axis=-1, keepdims=True)).astype(jnp.bfloat16)


def zonal_attend(query_rows, key_rows, value_rows):
    item_count, length, pair_width = query_rows.shape
    score_scale = HD ** (-0.5)
    query_heads = query_rows.reshape(item_count, length, 2, HD)
    key_heads = key_rows.reshape(item_count, length, 2, HD)
    value_heads = value_rows.reshape(item_count, length, 2, HD)
    block_rows = min(512, length)
    pieces = []
    for first_row in range(0, length, block_rows):
        query_block = query_heads[:, first_row : first_row + block_rows]
        scores = (
            jnp.einsum(
                "iqhd,ikhd->ihqk", query_block, key_heads, preferred_element_type=jnp.float32
            )
            * score_scale
        )
        soft_weights = softmax_rows(scores)
        result = jnp.einsum(
            "ihqk,ikhd->iqhd", soft_weights, value_heads, preferred_element_type=jnp.float32
        )
        pieces.append(result.astype(jnp.bfloat16))
    return jnp.concatenate(pieces, axis=1).reshape(item_count, length, pair_width)


def on_device(field, norm_gain, w_qkv, w_out, block_cols, antipode):
    cycle_count, lon_count, channels = field.shape
    column_heads = HEADS - HZ
    pair_count = HZ // 2
    zonal_width = HZ * HD
    score_scale = HD ** (-0.5)
    values = field.astype(jnp.float32)
    scaled = values * lax.rsqrt(jnp.mean(values * values, axis=-1, keepdims=True) + epsilon)
    normed = (scaled * norm_gain).astype(jnp.bfloat16)
    weight_split = w_qkv.reshape(channels, 3, channels)
    zonal_weight = weight_split[:, :, :zonal_width].reshape(channels, 3, pair_count, 2 * HD)
    column_weight = weight_split[:, :, zonal_width:]
    zonal_part = jnp.einsum(
        "rld,dtpc->trplc", normed, zonal_weight, preferred_element_type=jnp.float32
    )
    zonal_part = zonal_part.astype(jnp.bfloat16).reshape(
        3, cycle_count * pair_count, lon_count, 2 * HD
    )
    column_proj = jnp.einsum(
        "rld,dtc->rltc", normed, column_weight, preferred_element_type=jnp.float32
    ).astype(jnp.bfloat16)
    query_all, key_all, value_all = (
        lax.all_to_all(zonal_part[0], "lon", split_axis=0, concat_axis=1, tiled=True),
        lax.all_to_all(zonal_part[1], "lon", split_axis=0, concat_axis=1, tiled=True),
        lax.all_to_all(zonal_part[2], "lon", split_axis=0, concat_axis=1, tiled=True),
    )
    zonal_items = zonal_attend(query_all, key_all, value_all)
    returned = lax.all_to_all(zonal_items, "lon", split_axis=1, concat_axis=0, tiled=True)
    zonal_out = returned.reshape(cycle_count, pair_count, lon_count, 2 * HD)
    cap_half = lax.axis_index("lat") % 2
    lon_devices = lax.axis_size("lon")
    merged = column_proj[:, :, 1:]

    def cap_order(own_rows, other_rows):
        return jnp.where(
            cap_half == 0,
            jnp.concatenate([own_rows, other_rows], axis=0),
            jnp.concatenate([other_rows, own_rows], axis=0),
        )

    far_own = shifted(merged, "lon", lon_devices // 2)
    partner, far_partner = from_partner((merged, far_own), "lat", 0)
    cap_rows = cap_order(merged, partner)
    far_side = cap_order(far_own, far_partner)
    across = jnp.take(far_side, antipode % lon_count, axis=1)[::-1]
    column = jnp.concatenate([across, cap_rows], axis=0)
    block_total = column.shape[0] // BM
    column = column.reshape(block_total, BM, lon_count, 2, column_heads, HD)
    picks_per_row = block_cols.shape[1]
    local_blocks = cycle_count // BM
    pieces = []
    for local_block in range(local_blocks):
        block_row = cap_half * local_blocks + local_block
        picked = lax.dynamic_index_in_dim(block_cols, block_row, 0, keepdims=False)
        chosen = jnp.take(column, picked, axis=0).reshape(
            picks_per_row * BM, lon_count, 2, column_heads, HD
        )
        query_block = column_proj[local_block * BM : (local_block + 1) * BM, :, 0]
        query_block = query_block.reshape(BM, lon_count, column_heads, HD)
        scores = (
            jnp.einsum(
                "qlhd,klhd->lhqk", query_block, chosen[:, :, 0], preferred_element_type=jnp.float32
            )
            * score_scale
        )
        soft_weights = softmax_rows(scores)
        result = jnp.einsum(
            "lhqk,klhd->qlhd", soft_weights, chosen[:, :, 1], preferred_element_type=jnp.float32
        )
        pieces.append(result.astype(jnp.bfloat16).reshape(BM, lon_count, column_heads * HD))
    meridional = jnp.concatenate(pieces, axis=0)
    zonal_rows_out = w_out[:zonal_width].reshape(pair_count, 2 * HD, channels)
    total = jnp.einsum(
        "rplc,pce->rle", zonal_out, zonal_rows_out, preferred_element_type=jnp.float32
    )
    total = total + jnp.einsum(
        "rlc,ce->rle", meridional, w_out[zonal_width:], preferred_element_type=jnp.float32
    )
    return total.astype(jnp.bfloat16)


GROUP = 4
MESH = pl.DeviceIdType.MESH


def norm_rows(x, gain):
    values = x.astype(jnp.float32)
    mean = jnp.mean(values * values, axis=-1, keepdims=True)
    return (values * lax.rsqrt(mean + epsilon) * gain).astype(jnp.bfloat16)


def mm(a, b):
    return jnp.dot(a, b, preferred_element_type=jnp.float32).astype(jnp.bfloat16)


def pair_attend(q, k, v, mask):
    rows = q.shape[0]
    first = lax.broadcasted_iota(jnp.int32, q.shape, 1) < HD
    q = q * jnp.asarray(HD ** (-0.5), q.dtype)
    zero = jnp.zeros_like(q)
    stacked = jnp.concatenate([jnp.where(first, q, zero), jnp.where(first, zero, q)], axis=0)
    scores = lax.dot_general(stacked, k, (((1,), (1,)), ((), ())), preferred_element_type=jnp.float32)
    if mask is not None:
        scores = jnp.where(mask, scores, -jnp.inf)
    exponent = jnp.exp(scores - jnp.max(scores, axis=-1, keepdims=True))
    weights = (exponent * (1.0 / jnp.sum(exponent, axis=-1, keepdims=True))).astype(jnp.bfloat16)
    out = jnp.dot(weights, v, preferred_element_type=jnp.float32)
    return jnp.where(first, out[:rows], out[rows:]).astype(jnp.bfloat16)


def one_hot(hit):
    return jnp.where(hit, 1.0, 0.0).astype(jnp.bfloat16)


def iota(shape, axis):
    return lax.broadcasted_iota(jnp.int32, shape, axis)


def rows_at(start, size, step=None):
    return pl.ds(pl.multiple_of(start, step or size), size)


def layer_kernel(
    block_cols, ant_ref, gain_ref, x_hbm, w_hbm, wo_hbm, out_ref,
    xo, part, far, farpart, xz, w, wo, xn, kc, vc, qc, kz, vz, qz, zo, zret, oc, place, place_far,
    send, recv, local,
):
    lat, lon = lax.axis_index("lat"), lax.axis_index("lon")
    half, q = lon // GROUP, lon % GROUP
    cap_half = lat % 2
    anti = (1 - half) * GROUP + q
    mate = lat + 1 - 2 * cap_half
    steps, lons, width = x_hbm.shape[1:]
    side = HZ * HD
    span = GROUP * lons
    block = BM * lons
    blocks = GROUP * steps // BM
    groups = lons // 8
    gain = gain_ref[...]

    def peer(k):
        return lax.rem(q + k, GROUP)

    def remote(src, dst, n, lat_id, lon_id):
        return pltpu.make_async_remote_copy(
            src_ref=src,
            dst_ref=dst,
            send_sem=send.at[n],
            recv_sem=recv.at[n],
            device_id=(lat_id, lon_id),
            device_id_type=MESH,
        )

    def to_peer(src, dst, n, k):
        return remote(src, dst, n, lat, half * GROUP + peer(k))

    def far_copy(j):
        return remote(x_hbm.at[:, j], far.at[:, j], j, lat, anti)

    def near_copy(k):
        return to_peer(x_hbm.at[peer(k)], xz.at[:, 0, q], 3 + k, k)

    def pass_copy(j, k):
        return to_peer(far.at[peer(k), j], xz.at[j, 1, q], 8 + 3 * j + k - 1, k)

    def mate_copy(j):
        return remote(far.at[:, j], farpart.at[:, j], 20 + j, mate, lon)

    def back_copy(j, k):
        return to_peer(zo.at[j, peer(k)], zret.at[q, j], 24 + 3 * j + k - 1, k)

    def own_pass(j):
        return pltpu.make_async_copy(far.at[q, j], xz.at[j, 1, q], local.at[4 + j])

    def own_back(j):
        return pltpu.make_async_copy(zo.at[j, q], zret.at[q, j], local.at[8 + j])

    others = (1, 2, 3)
    barrier = pltpu.get_barrier_semaphore()
    partners = [(lat, anti), (mate, lon)] + [(lat, half * GROUP + peer(k)) for k in others]
    for a, b in partners:
        pl.semaphore_signal(barrier, inc=1, device_id=(a, b), device_id_type=MESH)
    load_x = pltpu.make_async_copy(x_hbm, xo, local.at[0])
    load_w = pltpu.make_async_copy(w_hbm, w, local.at[1])
    load_wo = pltpu.make_async_copy(wo_hbm, wo, local.at[2])
    own_near = pltpu.make_async_copy(x_hbm.at[q], xz.at[:, 0, q], local.at[3])
    load_x.start()
    load_w.start()
    pl.semaphore_wait(barrier, len(partners))
    for j in range(steps):
        far_copy(j).start()
    pair = remote(x_hbm, part, 7, mate, lon)
    pair.start()
    for k in others:
        near_copy(k).start()
    own_near.start()
    load_wo.start()

    def weight(which, zone):
        first = which * width + zone * side
        return w[:, first : first + side]

    token, slot = iota((block, block), 1), iota((block, block), 0)
    want = (slot // 8 % BM) * lons + (slot // (8 * BM)) * 8 + slot % 8
    place[...] = one_hot(token == want)
    perm = lax.rem(ant_ref[...], lons)
    lon_hot = one_hot(iota((lons, lons), 0) == perm)
    t = iota((span, lons), 0)
    spread = one_hot((t // 16 % groups) * 8 + t % 8 == iota((span, lons), 1))
    moved = lax.dot_general(spread, lon_hot, (((1,), (1,)), ((), ())), preferred_element_type=jnp.float32)
    tile = one_hot(iota((lons, span), 0) == iota((lons, span), 1) % lons)
    wide = jnp.dot(moved.astype(jnp.bfloat16), tile, preferred_element_type=jnp.float32)
    t, src = iota((span, span), 0), iota((span, span), 1)
    same = 2 * (t // (16 * groups)) + t // 8 % 2 == src // lons
    place_far[...] = jnp.where(same, wide, 0.0).astype(jnp.bfloat16)

    def column_source(ref, s):
        @pl.loop(0, blocks)
        def _(i):
            for c in range(0, BM, 2):
                piece = ref[i * (BM // steps) + c // steps, pl.ds(c % steps, 2)]
                xn[c * lons : (c + 2) * lons, :] = norm_rows(piece.reshape(2 * lons, width), gain)
            placed = mm(place[...], xn[0:block, :])
            to = rows_at((s * blocks + i) * block, block)
            kc[to, :] = mm(placed, weight(1, 1))
            vc[to, :] = mm(placed, weight(2, 1))
            if s == 0:
                qc[rows_at(i * block, block), :] = mm(placed, weight(0, 1))

    load_x.wait()
    load_w.wait()
    column_source(xo, 0)
    pair.wait_recv()
    column_source(part, 1)
    for k in others:
        near_copy(k).wait_recv()
    own_near.wait()

    def cycle_norm(j, h):
        for m in range(0, GROUP, 2):
            piece = xz[j, h, pl.ds(m, 2)].reshape(2 * lons, width)
            xn[m * lons : (m + 2) * lons, :] = norm_rows(piece, gain)

    def arrive(j):
        far_copy(j).wait_recv()
        for k in others:
            pass_copy(j, k).start()
        own_pass(j).start()
        mate_copy(j).start()

    arrive(0)

    @pl.loop(0, steps)
    def _(j):
        cycle_norm(j, 0)
        placed = xn[0:span, :]
        kz[j, 0:span, :] = mm(placed, weight(1, 0))
        vz[j, 0:span, :] = mm(placed, weight(2, 0))
        qz[j] = mm(placed, weight(0, 0))

    @pl.loop(0, steps)
    def _(j):
        @pl.when(j > 0)
        def _():
            arrive(j)
            for k in others:
                back_copy(j - 1, k).start()
            own_back(j - 1).start()

        mate_copy(j).wait_recv()
        for s, ref in ((0, far), (1, farpart)):
            for p in range(0, GROUP, 2):
                piece = ref[pl.ds(p, 2), j].reshape(2 * lons, width)
                xn[s * span + p * lons : s * span + (p + 2) * lons, :] = norm_rows(piece, gain)
        placed = jnp.concatenate(
            [mm(place_far[...], xn[0:span, :]), mm(place_far[...], xn[span : 2 * span, :])], axis=0
        )
        for which, ref in ((1, kc), (2, vc)):
            made = mm(placed, weight(which, 1))
            for n in range(2 * blocks * groups):
                to = rows_at((2 * blocks * groups + n) * 8 * BM + j * 16, 16)
                ref[to, :] = made[n * 16 : (n + 1) * 16]
        for k in others:
            pass_copy(j, k).wait_recv()
        own_pass(j).wait()
        cycle_norm(j, 1)
        placed = xn[0:span, :]
        kz[j, span : 2 * span, :] = mm(placed, weight(1, 0))
        vz[j, span : 2 * span, :] = mm(placed, weight(2, 0))
        for p in range(side // 128):
            cols = slice(p * 128, (p + 1) * 128)
            out = pair_attend(qz[j, :, cols], kz[j, :, cols], vz[j, :, cols], None)
            zo[j, :, :, cols] = out.reshape(GROUP, lons, 128)

    rows = 8 * BM
    mask = iota((2 * rows, 4 * rows), 0) % 8 == iota((2 * rows, 4 * rows), 1) % 8

    @pl.loop(0, blocks * groups)
    def _(n):
        @pl.when(n == 1)
        def _():
            for k in others:
                back_copy(steps - 1, k).start()
            own_back(steps - 1).start()

        b, g = n // groups, lax.rem(n, groups)
        first = 2 * blocks
        held = [cap_half * blocks + i for i in range(blocks)]
        held += [(1 - cap_half) * blocks + i for i in range(blocks)]
        held = [first + c for c in held] + [first - 1 - c for c in held]
        picks = [block_cols[cap_half * blocks + b, m] for m in range(4)]
        chosen = [[pick == name for name in held] for pick in picks]
        at = rows_at(n * rows, rows)

        def selected(ref, cols):
            pieces = [ref[rows_at((s * groups + g) * rows, rows), cols] for s in range(2 * first)]
            parts = []
            for flags in chosen:
                result = pieces[0]
                for flag, piece in zip(flags[1:], pieces[1:]):
                    result = lax.select_n(flag, result, piece)
                parts.append(result)
            return jnp.concatenate(parts, axis=0)

        for p in range(side // 128):
            cols = slice(p * 128, (p + 1) * 128)
            oc[at, cols] = pair_attend(qc[at, cols], selected(kc, cols), selected(vc, cols), mask)

    for j in range(steps):
        for k in others:
            back_copy(j, k).wait_recv()
        own_back(j).wait()
    load_wo.wait()

    @pl.loop(0, blocks)
    def _(i):
        at = rows_at(i * block, block)
        column = lax.dot_general(
            place[...], oc[at, :], (((0,), (0,)), ((), ())), preferred_element_type=jnp.float32
        ).astype(jnp.bfloat16)
        many = BM // steps
        zonal = zret[pl.ds(i * many, many)].reshape(block, side)
        total = jnp.dot(zonal, wo[0:side, :], preferred_element_type=jnp.float32)
        total += jnp.dot(column, wo[side : 2 * side, :], preferred_element_type=jnp.float32)
        out_ref[at, :] = total.astype(jnp.bfloat16)

    for j in range(steps):
        far_copy(j).wait_send()
        mate_copy(j).wait_send()
        for k in others:
            pass_copy(j, k).wait_send()
            back_copy(j, k).wait_send()
    pair.wait_send()
    for k in others:
        near_copy(k).wait_send()


def on_device_halves(field, norm_gain, w_qkv, w_out, block_cols, antipode):
    cycles, lons, width = field.shape
    tokens = cycles * lons
    steps = cycles // GROUP
    side = HZ * HD
    span = GROUP * lons
    block = BM * lons
    bf = jnp.bfloat16
    anywhere = pl.BlockSpec(memory_space=pl.ANY)
    vmem = pl.BlockSpec(memory_space=pltpu.VMEM)
    shapes = [
        (GROUP, steps, lons, width),
        (GROUP, steps, lons, width),
        (GROUP, steps, lons, width),
        (GROUP, steps, lons, width),
        (steps, 2, GROUP, lons, width),
        (width, 3 * width),
        (width, width),
        (2 * block, width),
        (4 * tokens, side),
        (4 * tokens, side),
        (tokens, side),
        (steps, 2 * span, side),
        (steps, 2 * span, side),
        (steps, span, side),
        (steps, GROUP, lons, side),
        (GROUP, steps, lons, side),
        (tokens, side),
        (block, block),
        (span, span),
    ]
    out = pl.pallas_call(
        layer_kernel,
        name="layer",
        out_shape=jax.ShapeDtypeStruct((tokens, width), bf),
        in_specs=[pl.BlockSpec(memory_space=pltpu.SMEM), vmem, vmem, anywhere, anywhere, anywhere],
        out_specs=vmem,
        scratch_shapes=[pltpu.VMEM(shape, bf) for shape in shapes]
        + [
            pltpu.SemaphoreType.DMA((36,)),
            pltpu.SemaphoreType.DMA((36,)),
            pltpu.SemaphoreType.DMA((12,)),
        ],
        compiler_params=pltpu.CompilerParams(
            collective_id=0, has_side_effects=True, vmem_limit_bytes=56 * 1024 * 1024
        ),
    )(
        block_cols,
        antipode.reshape(1, lons),
        norm_gain.reshape(1, width),
        field.reshape(GROUP, steps, lons, width),
        w_qkv,
        w_out,
    )
    return out.reshape(cycles, lons, width)


def solution(mesh):
    in_specs = (P("lat", "lon", None), P(), P(), P(), P(), P("lon"))
    out_specs = P("lat", "lon", None)
    halves = mesh.shape["lat"] == 4 and mesh.shape["lon"] == 2 * GROUP
    return jax.shard_map(
        on_device_halves if halves else on_device,
        mesh=mesh,
        in_specs=in_specs,
        out_specs=out_specs,
        check_vma=False,
    )
```

```python
import functools

import jax
import jax.numpy as jnp
from jax import lax
from jax.experimental import pallas as pl
from jax.experimental.pallas import tpu as pltpu
from jax.sharding import PartitionSpec as P

HEADS = 16
HD = 64
HZ = 8
BM = 8


epsilon = 1e-06


def shifted(shard, axis, by):
    devices = lax.axis_size(axis)
    return lax.ppermute(shard, axis, [(i, (i + by) % devices) for i in range(devices)])


def from_partner(value, axis, distance):
    mask = 2**distance
    pairs = [(source, source ^ mask) for source in range(lax.axis_size(axis))]
    return lax.ppermute(value, axis, pairs)


def softmax_rows(scores):
    row_max = jnp.max(scores, axis=-1, keepdims=True)
    exponent = jnp.exp(scores - row_max)
    return (exponent / jnp.sum(exponent, axis=-1, keepdims=True)).astype(jnp.bfloat16)


def zonal_attend(query_rows, key_rows, value_rows):
    item_count, length, pair_width = query_rows.shape
    score_scale = HD ** (-0.5)
    query_heads = query_rows.reshape(item_count, length, 2, HD)
    key_heads = key_rows.reshape(item_count, length, 2, HD)
    value_heads = value_rows.reshape(item_count, length, 2, HD)
    block_rows = min(512, length)
    pieces = []
    for first_row in range(0, length, block_rows):
        query_block = query_heads[:, first_row : first_row + block_rows]
        scores = (
            jnp.einsum(
                "iqhd,ikhd->ihqk", query_block, key_heads, preferred_element_type=jnp.float32
            )
            * score_scale
        )
        soft_weights = softmax_rows(scores)
        result = jnp.einsum(
            "ihqk,ikhd->iqhd", soft_weights, value_heads, preferred_element_type=jnp.float32
        )
        pieces.append(result.astype(jnp.bfloat16))
    return jnp.concatenate(pieces, axis=1).reshape(item_count, length, pair_width)


def on_device(field, norm_gain, w_qkv, w_out, block_cols, antipode):
    cycle_count, lon_count, channels = field.shape
    column_heads = HEADS - HZ
    pair_count = HZ // 2
    zonal_width = HZ * HD
    score_scale = HD ** (-0.5)
    values = field.astype(jnp.float32)
    scaled = values * lax.rsqrt(jnp.mean(values * values, axis=-1, keepdims=True) + epsilon)
    normed = (scaled * norm_gain).astype(jnp.bfloat16)
    weight_split = w_qkv.reshape(channels, 3, channels)
    zonal_weight = weight_split[:, :, :zonal_width].reshape(channels, 3, pair_count, 2 * HD)
    column_weight = weight_split[:, :, zonal_width:]
    zonal_part = jnp.einsum(
        "rld,dtpc->trplc", normed, zonal_weight, preferred_element_type=jnp.float32
    )
    zonal_part = zonal_part.astype(jnp.bfloat16).reshape(
        3, cycle_count * pair_count, lon_count, 2 * HD
    )
    column_proj = jnp.einsum(
        "rld,dtc->rltc", normed, column_weight, preferred_element_type=jnp.float32
    ).astype(jnp.bfloat16)
    query_all, key_all, value_all = (
        lax.all_to_all(zonal_part[0], "lon", split_axis=0, concat_axis=1, tiled=True),
        lax.all_to_all(zonal_part[1], "lon", split_axis=0, concat_axis=1, tiled=True),
        lax.all_to_all(zonal_part[2], "lon", split_axis=0, concat_axis=1, tiled=True),
    )
    zonal_items = zonal_attend(query_all, key_all, value_all)
    returned = lax.all_to_all(zonal_items, "lon", split_axis=1, concat_axis=0, tiled=True)
    zonal_out = returned.reshape(cycle_count, pair_count, lon_count, 2 * HD)
    cap_half = lax.axis_index("lat") % 2
    lon_devices = lax.axis_size("lon")
    merged = column_proj[:, :, 1:]

    def cap_order(own_rows, other_rows):
        return jnp.where(
            cap_half == 0,
            jnp.concatenate([own_rows, other_rows], axis=0),
            jnp.concatenate([other_rows, own_rows], axis=0),
        )

    far_own = shifted(merged, "lon", lon_devices // 2)
    partner, far_partner = from_partner((merged, far_own), "lat", 0)
    cap_rows = cap_order(merged, partner)
    far_side = cap_order(far_own, far_partner)
    across = jnp.take(far_side, antipode % lon_count, axis=1)[::-1]
    column = jnp.concatenate([across, cap_rows], axis=0)
    block_total = column.shape[0] // BM
    column = column.reshape(block_total, BM, lon_count, 2, column_heads, HD)
    picks_per_row = block_cols.shape[1]
    local_blocks = cycle_count // BM
    pieces = []
    for local_block in range(local_blocks):
        block_row = cap_half * local_blocks + local_block
        picked = lax.dynamic_index_in_dim(block_cols, block_row, 0, keepdims=False)
        chosen = jnp.take(column, picked, axis=0).reshape(
            picks_per_row * BM, lon_count, 2, column_heads, HD
        )
        query_block = column_proj[local_block * BM : (local_block + 1) * BM, :, 0]
        query_block = query_block.reshape(BM, lon_count, column_heads, HD)
        scores = (
            jnp.einsum(
                "qlhd,klhd->lhqk", query_block, chosen[:, :, 0], preferred_element_type=jnp.float32
            )
            * score_scale
        )
        soft_weights = softmax_rows(scores)
        result = jnp.einsum(
            "lhqk,klhd->qlhd", soft_weights, chosen[:, :, 1], preferred_element_type=jnp.float32
        )
        pieces.append(result.astype(jnp.bfloat16).reshape(BM, lon_count, column_heads * HD))
    meridional = jnp.concatenate(pieces, axis=0)
    zonal_rows_out = w_out[:zonal_width].reshape(pair_count, 2 * HD, channels)
    total = jnp.einsum(
        "rplc,pce->rle", zonal_out, zonal_rows_out, preferred_element_type=jnp.float32
    )
    total = total + jnp.einsum(
        "rlc,ce->rle", meridional, w_out[zonal_width:], preferred_element_type=jnp.float32
    )
    return total.astype(jnp.bfloat16)


GROUP = 4
MESH = pl.DeviceIdType.MESH


def norm_rows(x, gain):
    values = x.astype(jnp.float32)
    mean = jnp.mean(values * values, axis=-1, keepdims=True)
    return (values * lax.rsqrt(mean + epsilon) * gain).astype(jnp.bfloat16)


def mm(a, b):
    return jnp.dot(a, b, preferred_element_type=jnp.float32).astype(jnp.bfloat16)


def pair_attend(q, k, v, mask):
    rows = q.shape[0]
    first = lax.broadcasted_iota(jnp.int32, q.shape, 1) < HD
    q = q * jnp.asarray(HD ** (-0.5), q.dtype)
    zero = jnp.zeros_like(q)
    stacked = jnp.concatenate([jnp.where(first, q, zero), jnp.where(first, zero, q)], axis=0)
    scores = lax.dot_general(stacked, k, (((1,), (1,)), ((), ())), preferred_element_type=jnp.float32)
    if mask is not None:
        scores = jnp.where(mask, scores, -jnp.inf)
    exponent = jnp.exp(scores - jnp.max(scores, axis=-1, keepdims=True))
    weights = (exponent * (1.0 / jnp.sum(exponent, axis=-1, keepdims=True))).astype(jnp.bfloat16)
    out = jnp.dot(weights, v, preferred_element_type=jnp.float32)
    return jnp.where(first, out[:rows], out[rows:]).astype(jnp.bfloat16)


def one_hot(hit):
    return jnp.where(hit, 1.0, 0.0).astype(jnp.bfloat16)


def iota(shape, axis):
    return lax.broadcasted_iota(jnp.int32, shape, axis)


def rows_at(start, size, step=None):
    return pl.ds(pl.multiple_of(start, step or size), size)


def layer_kernel(
    block_cols, ant_ref, gain_ref, x_hbm, w_hbm, out_ref,
    xo, part, far, farpart, xz, w, xn, kc, vc, qc, kz, vz, qz, zo, zret, oc, place, place_far,
    send, recv, local,
):
    lat, lon = lax.axis_index("lat"), lax.axis_index("lon")
    half, q = lon // GROUP, lon % GROUP
    cap_half = lat % 2
    anti = (1 - half) * GROUP + q
    mate = lat + 1 - 2 * cap_half
    steps, lons, width = x_hbm.shape[1:]
    side = HZ * HD
    span = GROUP * lons
    block = BM * lons
    blocks = GROUP * steps // BM
    groups = lons // 8
    gain = gain_ref[...]

    def peer(k):
        return lax.rem(q + k, GROUP)

    def remote(src, dst, n, lat_id, lon_id):
        return pltpu.make_async_remote_copy(
            src_ref=src,
            dst_ref=dst,
            send_sem=send.at[n],
            recv_sem=recv.at[n],
            device_id=(lat_id, lon_id),
            device_id_type=MESH,
        )

    def to_peer(src, dst, n, k):
        return remote(src, dst, n, lat, half * GROUP + peer(k))

    def far_copy(j):
        return remote(x_hbm.at[:, j], far.at[:, j], j, lat, anti)

    def near_copy(k):
        return to_peer(x_hbm.at[peer(k)], xz.at[:, 0, q], 3 + k, k)

    def pass_copy(j, k):
        return to_peer(far.at[peer(k), j], xz.at[j, 1, q], 8 + 3 * j + k - 1, k)

    def mate_copy(j):
        return remote(far.at[:, j], farpart.at[:, j], 20 + j, mate, lon)

    def back_copy(j, k):
        return to_peer(zo.at[j, peer(k)], zret.at[q, j], 24 + 3 * j + k - 1, k)

    def own_pass(j):
        return pltpu.make_async_copy(far.at[q, j], xz.at[j, 1, q], local.at[4 + j])

    def own_back(j):
        return pltpu.make_async_copy(zo.at[j, q], zret.at[q, j], local.at[8 + j])

    others = (1, 2, 3)
    barrier = pltpu.get_barrier_semaphore()
    partners = [(lat, anti), (mate, lon)] + [(lat, half * GROUP + peer(k)) for k in others]
    for a, b in partners:
        pl.semaphore_signal(barrier, inc=1, device_id=(a, b), device_id_type=MESH)
    load_x = pltpu.make_async_copy(x_hbm, xo, local.at[0])
    load_w = pltpu.make_async_copy(w_hbm, w, local.at[1])
    own_near = pltpu.make_async_copy(x_hbm.at[q], xz.at[:, 0, q], local.at[3])
    load_x.start()
    load_w.start()
    pl.semaphore_wait(barrier, len(partners))
    pair = remote(x_hbm, part, 7, mate, lon)
    far_copy(0).start()
    far_copy(1).start()
    for k in others:
        near_copy(k).start()
    pair.start()
    own_near.start()

    def weight(which, zone):
        first = which * width + zone * side
        return w[:, first : first + side]

    token, slot = iota((block, block), 1), iota((block, block), 0)
    want = (slot // 8 % BM) * lons + (slot // (8 * BM)) * 8 + slot % 8
    place[...] = one_hot(token == want)
    perm = lax.rem(ant_ref[...], lons)
    lon_hot = one_hot(iota((lons, lons), 0) == perm)
    t = iota((span, lons), 0)
    spread = one_hot((t // 16 % groups) * 8 + t % 8 == iota((span, lons), 1))
    moved = lax.dot_general(spread, lon_hot, (((1,), (1,)), ((), ())), preferred_element_type=jnp.float32)
    tile = one_hot(iota((lons, span), 0) == iota((lons, span), 1) % lons)
    wide = jnp.dot(moved.astype(jnp.bfloat16), tile, preferred_element_type=jnp.float32)
    t, src = iota((span, span), 0), iota((span, span), 1)
    same = 2 * (t // (16 * groups)) + t // 8 % 2 == src // lons
    place_far[...] = jnp.where(same, wide, 0.0).astype(jnp.bfloat16)

    def column_source(ref, s):
        @pl.loop(0, blocks)
        def _(i):
            for c in range(0, BM, 2):
                piece = ref[i * (BM // steps) + c // steps, pl.ds(c % steps, 2)]
                xn[c * lons : (c + 2) * lons, :] = norm_rows(piece.reshape(2 * lons, width), gain)
            placed = mm(place[...], xn[0:block, :])
            to = rows_at((s * blocks + i) * block, block)
            kc[to, :] = mm(placed, weight(1, 1))
            vc[to, :] = mm(placed, weight(2, 1))
            if s == 0:
                qc[rows_at(i * block, block), :] = mm(placed, weight(0, 1))

    load_x.wait()
    load_w.wait()
    column_source(xo, 0)
    pair.wait_recv()
    column_source(part, 1)
    for k in others:
        near_copy(k).wait_recv()
    own_near.wait()

    def cycle_norm(j, h):
        for m in range(0, GROUP, 2):
            piece = xz[j, h, pl.ds(m, 2)].reshape(2 * lons, width)
            xn[m * lons : (m + 2) * lons, :] = norm_rows(piece, gain)

    def arrive(j):
        far_copy(j).wait_recv()
        for k in others:
            pass_copy(j, k).start()
        own_pass(j).start()
        mate_copy(j).start()

        @pl.when(j + 2 < steps)
        def _():
            far_copy(j + 2).start()


    arrive(0)

    @pl.loop(0, steps)
    def _(j):
        cycle_norm(j, 0)
        placed = xn[0:span, :]
        kz[j, 0:span, :] = mm(placed, weight(1, 0))
        vz[j, 0:span, :] = mm(placed, weight(2, 0))
        qz[j] = mm(placed, weight(0, 0))

    @pl.loop(0, steps)
    def _(j):
        @pl.when(j > 0)
        def _():
            arrive(j)
            for k in others:
                back_copy(j - 1, k).start()
            own_back(j - 1).start()

        mate_copy(j).wait_recv()
        for s, ref in ((0, far), (1, farpart)):
            for p in range(0, GROUP, 2):
                piece = ref[pl.ds(p, 2), j].reshape(2 * lons, width)
                xn[s * span + p * lons : s * span + (p + 2) * lons, :] = norm_rows(piece, gain)
        placed = jnp.concatenate(
            [mm(place_far[...], xn[0:span, :]), mm(place_far[...], xn[span : 2 * span, :])], axis=0
        )
        for which, ref in ((1, kc), (2, vc)):
            made = mm(placed, weight(which, 1))
            for n in range(2 * blocks * groups):
                to = rows_at((2 * blocks * groups + n) * 8 * BM + j * 16, 16)
                ref[to, :] = made[n * 16 : (n + 1) * 16]
        for k in others:
            pass_copy(j, k).wait_recv()
        own_pass(j).wait()
        cycle_norm(j, 1)
        placed = xn[0:span, :]
        kz[j, span : 2 * span, :] = mm(placed, weight(1, 0))
        vz[j, span : 2 * span, :] = mm(placed, weight(2, 0))
        for p in range(side // 128):
            cols = slice(p * 128, (p + 1) * 128)
            out = pair_attend(qz[j, :, cols], kz[j, :, cols], vz[j, :, cols], None)
            zo[j, :, :, cols] = out.reshape(GROUP, lons, 128)

    rows = 8 * BM
    mask = iota((2 * rows, 4 * rows), 0) % 8 == iota((2 * rows, 4 * rows), 1) % 8

    @pl.loop(0, blocks * groups)
    def _(n):
        @pl.when(n == 1)
        def _():
            for k in others:
                back_copy(steps - 1, k).start()
            own_back(steps - 1).start()

        b, g = n // groups, lax.rem(n, groups)
        first = 2 * blocks
        held = [cap_half * blocks + i for i in range(blocks)]
        held += [(1 - cap_half) * blocks + i for i in range(blocks)]
        held = [first + c for c in held] + [first - 1 - c for c in held]
        picks = [block_cols[cap_half * blocks + b, m] for m in range(4)]
        chosen = [[pick == name for name in held] for pick in picks]
        at = rows_at(n * rows, rows)

        def selected(ref, cols):
            pieces = [ref[rows_at((s * groups + g) * rows, rows), cols] for s in range(2 * first)]
            parts = []
            for flags in chosen:
                result = pieces[0]
                for flag, piece in zip(flags[1:], pieces[1:]):
                    result = lax.select_n(flag, result, piece)
                parts.append(result)
            return jnp.concatenate(parts, axis=0)

        for p in range(side // 128):
            cols = slice(p * 128, (p + 1) * 128)
            oc[at, cols] = pair_attend(qc[at, cols], selected(kc, cols), selected(vc, cols), mask)

    for j in range(steps):
        for k in others:
            back_copy(j, k).wait_recv()
        own_back(j).wait()

    @pl.loop(0, blocks)
    def _(i):
        at = rows_at(i * block, block)
        column = lax.dot_general(
            place[...], oc[at, :], (((0,), (0,)), ((), ())), preferred_element_type=jnp.float32
        ).astype(jnp.bfloat16)
        many = BM // steps
        zonal = zret[pl.ds(i * many, many)].reshape(block, side)
        out_ref[at, 0:side] = zonal
        out_ref[at, side : 2 * side] = column

    for j in range(steps):
        far_copy(j).wait_send()
        mate_copy(j).wait_send()
        for k in others:
            pass_copy(j, k).wait_send()
            back_copy(j, k).wait_send()
    pair.wait_send()
    for k in others:
        near_copy(k).wait_send()


def on_device_halves(field, norm_gain, w_qkv, w_out, block_cols, antipode):
    cycles, lons, width = field.shape
    tokens = cycles * lons
    steps = cycles // GROUP
    side = HZ * HD
    span = GROUP * lons
    block = BM * lons
    bf = jnp.bfloat16
    anywhere = pl.BlockSpec(memory_space=pl.ANY)
    vmem = pl.BlockSpec(memory_space=pltpu.VMEM)
    shapes = [
        (GROUP, steps, lons, width),
        (GROUP, steps, lons, width),
        (GROUP, steps, lons, width),
        (GROUP, steps, lons, width),
        (steps, 2, GROUP, lons, width),
        (width, 3 * width),
        (2 * block, width),
        (4 * tokens, side),
        (4 * tokens, side),
        (tokens, side),
        (steps, 2 * span, side),
        (steps, 2 * span, side),
        (steps, span, side),
        (steps, GROUP, lons, side),
        (GROUP, steps, lons, side),
        (tokens, side),
        (block, block),
        (span, span),
    ]
    out = pl.pallas_call(
        layer_kernel,
        name="layer",
        out_shape=jax.ShapeDtypeStruct((tokens, 2 * side), bf),
        in_specs=[pl.BlockSpec(memory_space=pltpu.SMEM), vmem, vmem, anywhere, anywhere],
        out_specs=vmem,
        scratch_shapes=[pltpu.VMEM(shape, bf) for shape in shapes]
        + [
            pltpu.SemaphoreType.DMA((36,)),
            pltpu.SemaphoreType.DMA((36,)),
            pltpu.SemaphoreType.DMA((12,)),
        ],
        compiler_params=pltpu.CompilerParams(
            collective_id=0, has_side_effects=True, vmem_limit_bytes=56 * 1024 * 1024
        ),
    )(
        block_cols,
        antipode.reshape(1, lons),
        norm_gain.reshape(1, width),
        field.reshape(GROUP, steps, lons, width),
        w_qkv,
    )
    out = jnp.dot(out, w_out, preferred_element_type=jnp.float32).astype(bf)
    return out.reshape(cycles, lons, width)


def solution(mesh):
    in_specs = (P("lat", "lon", None), P(), P(), P(), P(), P("lon"))
    out_specs = P("lat", "lon", None)
    halves = mesh.shape["lat"] == 4 and mesh.shape["lon"] == 2 * GROUP
    return jax.shard_map(
        on_device_halves if halves else on_device,
        mesh=mesh,
        in_specs=in_specs,
        out_specs=out_specs,
        check_vma=False,
    )
```
